32 devices in a mesh: ka: 16 (over z, x, core), ga: 2 (over y).
Axes of the slice: x: 2, y: 2, z: 4, core: 2. Of those that a mesh axis runs over, the one named last changes fastest.
Arguments:
- pair_density: bfloat16 [128, 32, 12032], P('ka', None, 'ga'), may hold values from -6 to 6
- coulomb: float32 [12032], P('ga'), may hold values from 3e-05 to 0.003
Outputs:
- kernel: float32 [4096, 1280], P(('ka', 'ga'))
The draws below stay inside these ranges and needn't reach their ends.
All inputs are finite; a program needn't handle non-finite values.
Results may differ from the reference program's by a relative error of at most 0.0013.
Values may be sent and summed in bfloat16 or wider, within the bound.
A program may use at most 64 MiB of HBM per device.

```python
import math
import jax
import jax.numpy as jnp
from jax import lax

PAIRS = 32
G = 12032
K_DEV = 8
STEPS = 2
NK = 128
N_KA = 16


def shard_levels(key, extent, cuts, least, high):
    gain = 1.0
    for axis_at, shards_of in cuts:
        draws = jax.random.uniform(jax.random.fold_in(jax.random.fold_in(key, 6), axis_at), (shards_of,), jnp.float32, least / len(cuts), high / len(cuts))
        gain = gain * jnp.repeat(jnp.exp(draws), extent[axis_at] // shards_of).reshape((-1,) + (1,) * (len(extent) - 1 - axis_at))
    return gain


def scatter_about(rng, shape, scale, most, split=(), kind=jnp.bfloat16):
    values = jax.random.normal(rng, shape, jnp.float32) * scale
    if len(split) > 0:
        values = shard_levels(rng, shape, split, -0.22, 0.18) * values
    return jnp.clip(values, min=-most, max=most).astype(kind)


def setup_inputs(seed: int = 0) -> dict:
    key_list = jax.random.split(jax.random.key(seed), 3)
    return {
        "pair_density": scatter_about(key_list[0], (NK, PAIRS, G), 1.0, 6.0, ((0, 16), (2, 2))),
        "coulomb": jnp.clip(jnp.exp(math.log(0.003) - 4.6051702 * jax.random.uniform(key_list[1], (G,), jnp.float32) ** shard_levels(key_list[1], (G,), ((0, 2),), -0.2, 0.2)), 2.9999999242136255e-05, 0.003),
    }


def reference(pair_density, coulomb):
    width = K_DEV * PAIRS
    density = pair_density.reshape(N_KA, width, G)

    def one_shard(index):
        own = lax.dynamic_index_in_dim(density, index, 0, False).astype(jnp.float32)
        weighted = lax.optimization_barrier((own * coulomb[None, :]).astype(jnp.bfloat16)).astype(jnp.float32)
        blocks = []
        for step in range(STEPS, -1, -1):
            other_index = ((index - step) % N_KA).astype(jnp.int32)
            other = lax.dynamic_index_in_dim(density, other_index, 0, False).astype(jnp.float32)
            blocks.append(jnp.dot(weighted, other.T, precision=lax.Precision.HIGHEST))
        return jnp.stack(blocks)

    lower = lax.map(one_shard, jnp.arange(N_KA, dtype=jnp.int32))
    columns = [lower[:, position] for position in range(STEPS + 1)]
    for step in range(1, STEPS + 1):
        mirrored = jnp.roll(lower[:, STEPS - step], -step, axis=0)
        columns.append(jnp.swapaxes(mirrored, 1, 2))
    joined = jnp.concatenate(columns, axis=2)
    return joined.reshape(N_KA * width, (2 * STEPS + 1) * width)
```

```python
import functools

import jax
import jax.numpy as jnp
from jax import lax
from jax.experimental import pallas as pl
from jax.experimental.pallas import tpu as pltpu
from jax.sharding import PartitionSpec as P

LANES = 128
GROUP = 4
MESH = pl.DeviceIdType.MESH


def product(left, right):
    return lax.dot_general(
        left, right, (((1,), (1,)), ((), ())), preferred_element_type=jnp.float32
    )


def weigh(rows, scale):
    return (rows.astype(jnp.float32) * scale).astype(jnp.bfloat16)


def plan(tiles):
    piece = -(-tiles // GROUP)
    depth = 2 if piece % 2 == 0 else 1
    return piece, depth, piece // depth


def kernel(
    count, own_hbm, coulomb_ref, out_ref,
    own_ref, slab, sums, diag, got_core, got_half, half, got_x, got_diag, turned, got_turned,
    own_sem, local_sem, a2a_send, a2a_recv, fwd_send, fwd_recv,
    red_send, red_recv, turn_send, turn_recv,
):
    me = lax.axis_index("ka")
    side = lax.axis_index("ga")
    width, waves = own_ref.shape
    rows = width // 2
    tiles = waves // LANES
    piece, depth, chunks = plan(tiles)
    span = depth * LANES
    rank = lax.rem(me, GROUP)
    base = me - rank
    core = lax.rem(rank, 2)
    column = rank // 2
    up = lax.rem(me + GROUP, count)
    down = lax.rem(me + count - GROUP, count)
    partners = (
        2 * (1 - column) + core,
        2 * (1 - column) + 1 - core,
        2 * column + 1 - core,
    )

    def at(ka, ga):
        return {"ka": ka, "ga": ga}

    barrier = pltpu.get_barrier_semaphore()
    greeted = [at(base + p, side) for p in partners]
    greeted += [at(up, side), at(down, side), at(me, 1 - side)]
    for shift in (1, 2):
        for other in (0, 1):
            greeted.append(at(lax.rem(me + shift, count), other))
            greeted.append(at(lax.rem(me + count - shift, count), other))
    for target in greeted:
        pl.semaphore_signal(barrier, inc=1, device_id=target, device_id_type=MESH)

    def first_wave(r):
        return jnp.minimum(r * piece, tiles - piece) * LANES

    def remote(src, dst, send, recv, target):
        return pltpu.make_async_remote_copy(
            src_ref=src, dst_ref=dst, send_sem=send, recv_sem=recv,
            device_id=target, device_id_type=MESH,
        )

    def window(r, chunk):
        return pl.ds(pl.multiple_of(first_wave(r) + chunk * span, LANES), span)

    def spread(chunk, index):
        target = partners[index]
        return remote(
            own_hbm.at[:, window(target, chunk)], slab.at[chunk, 2 + rank],
            a2a_send.at[index, chunk], a2a_recv.at[index, chunk], at(base + target, side),
        )

    def local(chunk):
        return pltpu.make_async_copy(
            own_hbm.at[:, window(rank, chunk)], slab.at[chunk, 2 + rank], local_sem.at[chunk]
        )

    def forward(chunk):
        return remote(
            slab.at[chunk, pl.ds(GROUP, 2)], slab.at[chunk, pl.ds(0, 2)],
            fwd_send.at[chunk], fwd_recv.at[chunk], at(up, side),
        )

    whole = pltpu.make_async_copy(own_hbm, own_ref, own_sem)
    whole.start()
    for chunk in range(chunks):
        local(chunk).start()
    pl.semaphore_wait(barrier, len(greeted))
    for chunk in range(chunks):
        for index in range(3):
            spread(chunk, index).start()

    whole.wait()
    diag[...] = jnp.zeros_like(diag)

    def add_diag(start, size):
        mine = own_ref[:, pl.ds(start, size)]
        diag[...] += product(weigh(mine, coulomb_ref[:, pl.ds(start, size)]), mine)

    @pl.loop(0, tiles // 2)
    def _(step):
        add_diag(pl.multiple_of(step * 2 * LANES, LANES), 2 * LANES)

    if tiles % 2:
        add_diag((tiles - 1) * LANES, LANES)
    my_rows = pl.ds(pl.multiple_of(side * rows, rows), rows)
    their_rows = pl.ds(pl.multiple_of((1 - side) * rows, rows), rows)
    send_diag = remote(
        diag.at[their_rows], got_diag, red_send.at[3], red_recv.at[3], at(me, 1 - side)
    )
    send_diag.start()

    sums[...] = jnp.zeros_like(sums)

    def scale_of(chunk):
        start = first_wave(rank) + chunk * span
        scale = coulomb_ref[:, pl.ds(pl.multiple_of(start, LANES), span)]
        wave = start + lax.broadcasted_iota(jnp.int32, (1, span), 1)
        return jnp.where(wave >= rank * piece * LANES, scale, 0.0)

    def add_block(chunk, scale, shard, steps):
        left = weigh(slab[chunk, 2 + shard], scale)
        for step in steps:
            where = pl.ds((2 - step) * width, width)
            sums[shard % 2, shard // 2, :, where] += product(left, slab[chunk, 2 + shard - step])

    @pl.loop(0, chunks)
    def _(chunk):
        local(chunk).wait()
        for index in range(3):
            spread(chunk, index).wait_recv()
        forward(chunk).start()
        scale = scale_of(chunk)
        add_block(chunk, scale, 1, (1,))
        add_block(chunk, scale, 2, (2, 1))
        add_block(chunk, scale, 3, (2, 1))

    @pl.loop(0, chunks)
    def _(chunk):
        forward(chunk).wait_recv()
        scale = scale_of(chunk)
        add_block(chunk, scale, 0, (2, 1))
        add_block(chunk, scale, 1, (2,))

    to_core = remote(
        sums.at[1 - core], got_core, red_send.at[0], red_recv.at[0], at(base + partners[2], side)
    )
    to_core.start()
    to_core.wait()
    sums[core] += got_core[...]
    to_half = remote(
        sums.at[core, :, their_rows], got_half, red_send.at[1], red_recv.at[1], at(me, 1 - side)
    )
    to_half.start()
    to_half.wait()
    half[...] = sums[core, :, my_rows] + got_half[...]
    to_x = remote(
        half.at[1 - column], got_x, red_send.at[2], red_recv.at[2], at(base + partners[0], side)
    )
    to_x.start()
    to_x.wait()
    lower = half[column] + got_x[...]
    out_ref[:, 0 : 2 * width] = lower

    def turn(step, other):
        slot = (step - 1) * 2 + other
        return remote(
            turned.at[slot], got_turned.at[step - 1, side],
            turn_send.at[slot], turn_recv.at[step - 1, side],
            at(lax.rem(me + count - step, count), other),
        )

    for step in (2, 1):
        for other in (0, 1):
            begin = (2 - step) * width + other * rows
            turned[(step - 1) * 2 + other] = lower[:, begin : begin + rows].T
            turn(step, other).start()
    send_diag.wait()
    out_ref[:, 2 * width : 3 * width] = diag[my_rows, :] + got_diag[...]
    for step in (2, 1):
        for other in (0, 1):
            pltpu.make_async_copy(
                got_turned.at[step - 1, other], got_turned.at[step - 1, other],
                turn_recv.at[step - 1, other],
            ).wait()
            begin = (2 + step) * width + other * rows
            out_ref[:, begin : begin + rows] = got_turned[step - 1, other]
    for step in (2, 1):
        for other in (0, 1):
            turn(step, other).wait_send()

    @pl.loop(0, chunks)
    def _(chunk):
        forward(chunk).wait_send()
        for index in range(3):
            spread(chunk, index).wait_send()


def shards(count, pair_density, coulomb):
    shard_points, pairs, waves = pair_density.shape
    width = shard_points * pairs
    rows = width // 2
    piece, depth, chunks = plan(waves // LANES)
    span = depth * LANES
    wide = 2 * width
    dma = pltpu.SemaphoreType.DMA
    return pl.pallas_call(
        functools.partial(kernel, count),
        out_shape=jax.ShapeDtypeStruct((rows, 5 * width), jnp.float32),
        in_specs=[
            pl.BlockSpec(memory_space=pl.ANY),
            pl.BlockSpec(memory_space=pltpu.VMEM),
        ],
        out_specs=pl.BlockSpec(memory_space=pltpu.VMEM),
        scratch_shapes=[
            pltpu.VMEM((width, waves), jnp.bfloat16),
            pltpu.VMEM((chunks, GROUP + 2, width, span), jnp.bfloat16),
            pltpu.VMEM((2, 2, width, wide), jnp.float32),
            pltpu.VMEM((width, width), jnp.float32),
            pltpu.VMEM((2, width, wide), jnp.float32),
            pltpu.VMEM((2, rows, wide), jnp.float32),
            pltpu.VMEM((2, rows, wide), jnp.float32),
            pltpu.VMEM((rows, wide), jnp.float32),
            pltpu.VMEM((rows, width), jnp.float32),
            pltpu.VMEM((4, rows, rows), jnp.float32),
            pltpu.VMEM((2, 2, rows, rows), jnp.float32),
            dma, dma((chunks,)), dma((3, chunks)), dma((3, chunks)),
            dma((chunks,)), dma((chunks,)), dma((4,)), dma((4,)), dma((4,)), dma((2, 2)),
        ],
        compiler_params=pltpu.CompilerParams(
            collective_id=0, has_side_effects=True, vmem_limit_bytes=48 * 1024 * 1024
        ),
    )(pair_density.reshape(width, waves), coulomb.reshape(1, waves))


def solution(mesh):
    in_specs = (P("ka", None, "ga"), P("ga"))
    out_specs = P(("ka", "ga"), None)
    body = functools.partial(shards, mesh.shape["ka"])
    return jax.shard_map(body, mesh=mesh, in_specs=in_specs, out_specs=out_specs, check_vma=False)
```

```python
import functools

import jax
import jax.numpy as jnp
from jax import lax
from jax.experimental import pallas as pl
from jax.experimental.pallas import tpu as pltpu
from jax.sharding import PartitionSpec as P

LANES = 128
GROUP = 4
MESH = pl.DeviceIdType.MESH


def product(left, right):
    return lax.dot_general(
        left, right, (((1,), (1,)), ((), ())), preferred_element_type=jnp.float32
    )


def weigh(rows, scale):
    return (rows.astype(jnp.float32) * scale).astype(jnp.bfloat16)


def plan(tiles):
    piece = -(-tiles // GROUP)
    depth = 2 if piece % 2 == 0 else 1
    return piece, depth, piece // depth


def kernel(
    count, own_hbm, coulomb_ref, out_ref,
    own_ref, slab, sums, diag, got_core, got_half, half, got_x, got_diag, turned, got_turned,
    own_sem, local_sem, a2a_send, a2a_recv, fwd_send, fwd_recv,
    red_send, red_recv, turn_send, turn_recv,
):
    me = lax.axis_index("ka")
    side = lax.axis_index("ga")
    width, waves = own_ref.shape
    rows = width // 2
    tiles = waves // LANES
    piece, depth, chunks = plan(tiles)
    span = depth * LANES
    rank = lax.rem(me, GROUP)
    base = me - rank
    core = lax.rem(rank, 2)
    column = rank // 2
    up = lax.rem(me + GROUP, count)
    down = lax.rem(me + count - GROUP, count)
    partners = (
        2 * (1 - column) + core,
        2 * (1 - column) + 1 - core,
        2 * column + 1 - core,
    )

    def at(ka, ga):
        return {"ka": ka, "ga": ga}

    barrier = pltpu.get_barrier_semaphore()
    greeted = [at(base + p, side) for p in partners]
    greeted += [at(up, side), at(down, side), at(me, 1 - side)]
    for shift in (1, 2):
        for other in (0, 1):
            greeted.append(at(lax.rem(me + shift, count), other))
            greeted.append(at(lax.rem(me + count - shift, count), other))
    for target in greeted:
        pl.semaphore_signal(barrier, inc=1, device_id=target, device_id_type=MESH)

    def first_wave(r):
        return jnp.minimum(r * piece, tiles - piece) * LANES

    def remote(src, dst, send, recv, target):
        return pltpu.make_async_remote_copy(
            src_ref=src, dst_ref=dst, send_sem=send, recv_sem=recv,
            device_id=target, device_id_type=MESH,
        )

    def window(r, chunk):
        return pl.ds(pl.multiple_of(first_wave(r) + chunk * span, LANES), span)

    def spread(chunk, index):
        target = partners[index]
        return remote(
            own_hbm.at[:, window(target, chunk)], slab.at[chunk, 2 + rank],
            a2a_send.at[index, chunk], a2a_recv.at[index, chunk], at(base + target, side),
        )

    def local(chunk):
        return pltpu.make_async_copy(
            own_hbm.at[:, window(rank, chunk)], slab.at[chunk, 2 + rank], local_sem.at[chunk]
        )

    def forward(chunk):
        return remote(
            slab.at[chunk, pl.ds(GROUP, 2)], slab.at[chunk, pl.ds(0, 2)],
            fwd_send.at[chunk], fwd_recv.at[chunk], at(up, side),
        )

    whole = pltpu.make_async_copy(own_hbm, own_ref, own_sem)
    whole.start()
    for chunk in range(chunks):
        local(chunk).start()
    pl.semaphore_wait(barrier, len(greeted))
    for chunk in range(chunks):
        for index in range(3):
            spread(chunk, index).start()

    whole.wait()
    diag[...] = jnp.zeros_like(diag)

    def add_diag(start, size):
        mine = own_ref[:, pl.ds(start, size)]
        diag[...] += product(weigh(mine, coulomb_ref[:, pl.ds(start, size)]), mine)

    @pl.loop(0, tiles // 2)
    def _(step):
        add_diag(pl.multiple_of(step * 2 * LANES, LANES), 2 * LANES)

    if tiles % 2:
        add_diag((tiles - 1) * LANES, LANES)
    my_rows = pl.ds(pl.multiple_of(side * rows, rows), rows)
    their_rows = pl.ds(pl.multiple_of((1 - side) * rows, rows), rows)
    send_diag = remote(
        diag.at[their_rows], got_diag, red_send.at[10], red_recv.at[10], at(me, 1 - side)
    )
    send_diag.start()

    sums[...] = jnp.zeros_like(sums)

    def scale_of(chunk):
        start = first_wave(rank) + chunk * span
        scale = coulomb_ref[:, pl.ds(pl.multiple_of(start, LANES), span)]
        wave = start + lax.broadcasted_iota(jnp.int32, (1, span), 1)
        return jnp.where(wave >= rank * piece * LANES, scale, 0.0)

    def add_block(chunk, scale, shard, steps):
        left = weigh(slab[chunk, 2 + shard], scale)
        for step in steps:
            where = pl.ds((2 - step) * width, width)
            sums[shard % 2, shard // 2, :, where] += product(left, slab[chunk, 2 + shard - step])

    def arrive(chunk):
        local(chunk).wait()
        for index in range(3):
            spread(chunk, index).wait_recv()
        forward(chunk).start()
        scale = scale_of(chunk)
        add_block(chunk, scale, 1, (1,))
        add_block(chunk, scale, 2, (2, 1))
        add_block(chunk, scale, 3, (2, 1))

    def arrive_below(chunk):
        forward(chunk).wait_recv()
        scale = scale_of(chunk)
        add_block(chunk, scale, 0, (2, 1))
        add_block(chunk, scale, 1, (2,))

    def columns(step):
        return pl.ds((2 - step) * width, width)

    def to_core(pair, step):
        slot = pair * 2 + step - 1
        return remote(
            sums.at[1 - core, pair, :, columns(step)], got_core.at[pair, :, columns(step)],
            red_send.at[slot], red_recv.at[slot], at(base + partners[2], side),
        )

    def to_half(pair, step):
        slot = 4 + pair * 2 + step - 1
        return remote(
            sums.at[core, pair, their_rows, columns(step)], got_half.at[pair, :, columns(step)],
            red_send.at[slot], red_recv.at[slot], at(me, 1 - side),
        )

    def to_x(pair, step):
        slot = 8 + step - 1
        return remote(
            half.at[pair, :, columns(step)], got_x.at[:, columns(step)],
            red_send.at[slot], red_recv.at[slot], at(base + partners[0], side),
        )

    steps = (2, 1)

    def add_core(pair):
        for step in steps:
            to_core(pair, step).wait_recv()
            sums[core, pair, their_rows, columns(step)] += got_core[pair, their_rows, columns(step)]
            to_half(pair, step).start()
            sums[core, pair, my_rows, columns(step)] += got_core[pair, my_rows, columns(step)]

    def add_half(pair):
        for step in steps:
            to_half(pair, step).wait_recv()
            half[pair, :, columns(step)] = (
                sums[core, pair, my_rows, columns(step)] + got_half[pair, :, columns(step)]
            )

            @pl.when(column != pair)
            def _():
                to_x(pair, step).start()

    last = chunks - 1

    @pl.loop(0, last)
    def _(chunk):
        arrive(chunk)

        @pl.when(chunk > 0)
        def _():
            arrive_below(chunk - 1)

    arrive(last)
    for step in steps:
        to_core(1, step).start()
    if last > 0:
        arrive_below(last - 1)
    add_core(1)
    arrive_below(last)
    for step in steps:
        to_core(0, step).start()
    add_half(1)
    add_core(0)
    add_half(0)

    def turn(step, other):
        slot = (step - 1) * 2 + other
        return remote(
            turned.at[slot], got_turned.at[step - 1, side],
            turn_send.at[slot], turn_recv.at[step - 1, side],
            at(lax.rem(me + count - step, count), other),
        )

    for step in steps:
        to_x(0, step).wait_recv()
        lower = half[column, :, columns(step)] + got_x[:, columns(step)]
        for other in (0, 1):
            turned[(step - 1) * 2 + other] = lower[:, other * rows : (other + 1) * rows].T
            turn(step, other).start()
        out_ref[:, columns(step)] = lower
    send_diag.wait()
    out_ref[:, 2 * width : 3 * width] = diag[my_rows, :] + got_diag[...]
    for step in steps:
        for other in (0, 1):
            pltpu.make_async_copy(
                got_turned.at[step - 1, other], got_turned.at[step - 1, other],
                turn_recv.at[step - 1, other],
            ).wait()
            begin = (2 + step) * width + other * rows
            out_ref[:, begin : begin + rows] = got_turned[step - 1, other]
    for step in steps:
        for other in (0, 1):
            turn(step, other).wait_send()
    for step in steps:
        to_x(0, step).wait_send()
        for pair in (0, 1):
            to_core(pair, step).wait_send()
            to_half(pair, step).wait_send()

    @pl.loop(0, chunks)
    def _(chunk):
        forward(chunk).wait_send()
        for index in range(3):
            spread(chunk, index).wait_send()


def shards(count, pair_density, coulomb):
    shard_points, pairs, waves = pair_density.shape
    width = shard_points * pairs
    rows = width // 2
    piece, depth, chunks = plan(waves // LANES)
    span = depth * LANES
    wide = 2 * width
    dma = pltpu.SemaphoreType.DMA
    return pl.pallas_call(
        functools.partial(kernel, count),
        out_shape=jax.ShapeDtypeStruct((rows, 5 * width), jnp.float32),
        in_specs=[
            pl.BlockSpec(memory_space=pl.ANY),
            pl.BlockSpec(memory_space=pltpu.VMEM),
        ],
        out_specs=pl.BlockSpec(memory_space=pltpu.VMEM),
        scratch_shapes=[
            pltpu.VMEM((width, waves), jnp.bfloat16),
            pltpu.VMEM((chunks, GROUP + 2, width, span), jnp.bfloat16),
            pltpu.VMEM((2, 2, width, wide), jnp.float32),
            pltpu.VMEM((width, width), jnp.float32),
            pltpu.VMEM((2, width, wide), jnp.float32),
            pltpu.VMEM((2, rows, wide), jnp.float32),
            pltpu.VMEM((2, rows, wide), jnp.float32),
            pltpu.VMEM((rows, wide), jnp.float32),
            pltpu.VMEM((rows, width), jnp.float32),
            pltpu.VMEM((4, rows, rows), jnp.float32),
            pltpu.VMEM((2, 2, rows, rows), jnp.float32),
            dma, dma((chunks,)), dma((3, chunks)), dma((3, chunks)),
            dma((chunks,)), dma((chunks,)), dma((11,)), dma((11,)), dma((4,)), dma((2, 2)),
        ],
        compiler_params=pltpu.CompilerParams(
            collective_id=0, has_side_effects=True, vmem_limit_bytes=48 * 1024 * 1024
        ),
    )(pair_density.reshape(width, waves), coulomb.reshape(1, waves))


def solution(mesh):
    in_specs = (P("ka", None, "ga"), P("ga"))
    out_specs = P(("ka", "ga"), None)
    body = functools.partial(shards, mesh.shape["ka"])
    return jax.shard_map(body, mesh=mesh, in_specs=in_specs, out_specs=out_specs, check_vma=False)
```

```python
import functools

import jax
import jax.numpy as jnp
from jax import lax
from jax.experimental import pallas as pl
from jax.experimental.pallas import tpu as pltpu
from jax.sharding import PartitionSpec as P

LANES = 128
GROUP = 4
MESH = pl.DeviceIdType.MESH


def product(left, right):
    return lax.dot_general(
        left, right, (((1,), (1,)), ((), ())), preferred_element_type=jnp.float32
    )


def weigh(rows, scale):
    return (rows.astype(jnp.float32) * scale).astype(jnp.bfloat16)


def plan(tiles):
    piece = -(-tiles // GROUP)
    depth = 1
    return piece, depth, piece // depth


def kernel(
    count, own_hbm, coulomb_hbm, out_ref,
    coulomb_ref, own_ref, slab, sums, diag, got_core, got_half, half, got_x, got_diag, turned, got_turned,
    own_sem, coulomb_sem, local_sem, a2a_send, a2a_recv, fwd_send, fwd_recv,
    red_send, red_recv, turn_send, turn_recv,
):
    me = lax.axis_index("ka")
    side = lax.axis_index("ga")
    width, waves = own_ref.shape
    rows = width // 2
    tiles = waves // LANES
    piece, depth, chunks = plan(tiles)
    span = depth * LANES
    rank = lax.rem(me, GROUP)
    base = me - rank
    core = lax.rem(rank, 2)
    column = rank // 2
    up = lax.rem(me + GROUP, count)
    down = lax.rem(me + count - GROUP, count)
    partners = (
        2 * (1 - column) + core,
        2 * (1 - column) + 1 - core,
        2 * column + 1 - core,
    )

    def at(ka, ga):
        return {"ka": ka, "ga": ga}

    barrier = pltpu.get_barrier_semaphore()
    greeted = [at(base + p, side) for p in partners]
    greeted += [at(down, side), at(me, 1 - side)]
    for target in greeted:
        pl.semaphore_signal(barrier, inc=1, device_id=target, device_id_type=MESH)

    def first_wave(r):
        return jnp.minimum(r * piece, tiles - piece) * LANES

    def remote(src, dst, send, recv, target):
        return pltpu.make_async_remote_copy(
            src_ref=src, dst_ref=dst, send_sem=send, recv_sem=recv,
            device_id=target, device_id_type=MESH,
        )

    def window(r, chunk):
        return pl.ds(pl.multiple_of(first_wave(r) + chunk * span, LANES), span)

    def spread(chunk, index):
        target = partners[index]
        return remote(
            own_hbm.at[:, window(target, chunk)], slab.at[chunk, 2 + rank],
            a2a_send.at[index, chunk], a2a_recv.at[index, chunk], at(base + target, side),
        )

    def local(chunk):
        return pltpu.make_async_copy(
            own_hbm.at[:, window(rank, chunk)], slab.at[chunk, 2 + rank], local_sem.at[chunk]
        )

    def forward(chunk):
        return remote(
            slab.at[chunk, pl.ds(GROUP, 2)], slab.at[chunk, pl.ds(0, 2)],
            fwd_send.at[chunk], fwd_recv.at[chunk], at(up, side),
        )

    whole = pltpu.make_async_copy(own_hbm, own_ref, own_sem)
    whole.start()
    scales = pltpu.make_async_copy(coulomb_hbm, coulomb_ref.at[0], coulomb_sem)
    scales.start()
    for chunk in range(chunks):
        local(chunk).start()
    pl.semaphore_wait(barrier, len(greeted))
    for chunk in range(chunks):
        for index in range(3):
            spread(chunk, index).start()

    whole.wait()
    scales.wait()
    diag[...] = jnp.zeros_like(diag)

    def add_diag(start, size):
        mine = own_ref[:, pl.ds(start, size)]
        diag[...] += product(weigh(mine, coulomb_ref[:, pl.ds(start, size)]), mine)

    @pl.loop(0, tiles // 2)
    def _(step):
        add_diag(pl.multiple_of(step * 2 * LANES, LANES), 2 * LANES)

    if tiles % 2:
        add_diag((tiles - 1) * LANES, LANES)
    my_rows = pl.ds(pl.multiple_of(side * rows, rows), rows)
    their_rows = pl.ds(pl.multiple_of((1 - side) * rows, rows), rows)
    send_diag = remote(
        diag.at[their_rows], got_diag, red_send.at[20], red_recv.at[20], at(me, 1 - side)
    )
    send_diag.start()

    sums[...] = jnp.zeros_like(sums)

    def scale_of(chunk):
        start = first_wave(rank) + chunk * span
        scale = coulomb_ref[:, pl.ds(pl.multiple_of(start, LANES), span)]
        wave = start + lax.broadcasted_iota(jnp.int32, (1, span), 1)
        return jnp.where(wave >= rank * piece * LANES, scale, 0.0)

    def add_block(chunk, scale, shard, steps):
        left = weigh(slab[chunk, 2 + shard], scale)
        for step in steps:
            where = pl.ds((2 - step) * width, width)
            sums[shard % 2, shard // 2, :, where] += product(left, slab[chunk, 2 + shard - step])

    def arrive(chunk):
        local(chunk).wait()
        for index in range(3):
            spread(chunk, index).wait_recv()
        forward(chunk).start()
        scale = scale_of(chunk)
        add_block(chunk, scale, 1, (1,))
        add_block(chunk, scale, 2, (2, 1))
        add_block(chunk, scale, 3, (2, 1))

    def arrive_below(chunk):
        forward(chunk).wait_recv()
        scale = scale_of(chunk)
        add_block(chunk, scale, 0, (2, 1))
        add_block(chunk, scale, 1, (2,))

    def columns(part):
        return pl.ds(part * rows, rows)

    def to_core(pair, part):
        slot = pair * 4 + part
        return remote(
            sums.at[1 - core, pair, :, columns(part)], got_core.at[pair, :, columns(part)],
            red_send.at[slot], red_recv.at[slot], at(base + partners[2], side),
        )

    def to_half(pair, part):
        slot = 8 + pair * 4 + part
        return remote(
            sums.at[core, pair, their_rows, columns(part)], got_half.at[pair, :, columns(part)],
            red_send.at[slot], red_recv.at[slot], at(me, 1 - side),
        )

    def to_x(pair, part):
        slot = 16 + part
        return remote(
            half.at[pair, :, columns(part)], got_x.at[:, columns(part)],
            red_send.at[slot], red_recv.at[slot], at(base + partners[0], side),
        )

    parts = range(4)

    def add_core(pair):
        for part in parts:
            to_core(pair, part).wait_recv()
            sums[core, pair, their_rows, columns(part)] += got_core[pair, their_rows, columns(part)]
            to_half(pair, part).start()
            sums[core, pair, my_rows, columns(part)] += got_core[pair, my_rows, columns(part)]

    def add_half(pair):
        for part in parts:
            to_half(pair, part).wait_recv()
            half[pair, :, columns(part)] = (
                sums[core, pair, my_rows, columns(part)] + got_half[pair, :, columns(part)]
            )

            @pl.when(column != pair)
            def _():
                to_x(pair, part).start()

    last = chunks - 1

    @pl.loop(0, last)
    def _(chunk):
        arrive(chunk)

        @pl.when(chunk > 0)
        def _():
            arrive_below(chunk - 1)

    arrive(last)
    for part in parts:
        to_core(1, part).start()
    if last > 0:
        arrive_below(last - 1)
    add_core(1)
    arrive_below(last)
    for part in parts:
        to_core(0, part).start()
    add_half(1)
    add_core(0)
    add_half(0)

    def turn(step, other):
        slot = (step - 1) * 2 + other
        return remote(
            turned.at[slot], got_turned.at[step - 1, side],
            turn_send.at[slot], turn_recv.at[step - 1, side],
            at(lax.rem(me + count - step, count), other),
        )

    for part in parts:
        step, other = 2 - part // 2, part % 2
        to_x(0, part).wait_recv()
        lower = half[column, :, columns(part)] + got_x[:, columns(part)]
        turned[(step - 1) * 2 + other] = lower.T
        turn(step, other).start()
        out_ref[:, columns(part)] = lower
    send_diag.wait()
    out_ref[:, 2 * width : 3 * width] = diag[my_rows, :] + got_diag[...]
    for step in (2, 1):
        for other in (0, 1):
            pltpu.make_async_copy(
                got_turned.at[step - 1, other], got_turned.at[step - 1, other],
                turn_recv.at[step - 1, other],
            ).wait()
            begin = (2 + step) * width + other * rows
            out_ref[:, begin : begin + rows] = got_turned[step - 1, other]
    for step in (2, 1):
        for other in (0, 1):
            turn(step, other).wait_send()
    for part in parts:
        to_x(0, part).wait_send()
        for pair in (0, 1):
            to_core(pair, part).wait_send()
            to_half(pair, part).wait_send()

    @pl.loop(0, chunks)
    def _(chunk):
        forward(chunk).wait_send()
        for index in range(3):
            spread(chunk, index).wait_send()


def shards(count, pair_density, coulomb):
    shard_points, pairs, waves = pair_density.shape
    width = shard_points * pairs
    rows = width // 2
    piece, depth, chunks = plan(waves // LANES)
    span = depth * LANES
    wide = 2 * width
    dma = pltpu.SemaphoreType.DMA
    return pl.pallas_call(
        functools.partial(kernel, count),
        out_shape=jax.ShapeDtypeStruct((rows, 5 * width), jnp.float32),
        in_specs=[
            pl.BlockSpec(memory_space=pl.ANY),
            pl.BlockSpec(memory_space=pl.ANY),
        ],
        out_specs=pl.BlockSpec(memory_space=pltpu.VMEM),
        scratch_shapes=[
            pltpu.VMEM((1, waves), jnp.float32),
            pltpu.VMEM((width, waves), jnp.bfloat16),
            pltpu.VMEM((chunks, GROUP + 2, width, span), jnp.bfloat16),
            pltpu.VMEM((2, 2, width, wide), jnp.float32),
            pltpu.VMEM((width, width), jnp.float32),
            pltpu.VMEM((2, width, wide), jnp.float32),
            pltpu.VMEM((2, rows, wide), jnp.float32),
            pltpu.VMEM((2, rows, wide), jnp.float32),
            pltpu.VMEM((rows, wide), jnp.float32),
            pltpu.VMEM((rows, width), jnp.float32),
            pltpu.VMEM((4, rows, rows), jnp.float32),
            pltpu.VMEM((2, 2, rows, rows), jnp.float32),
            dma, dma, dma((chunks,)), dma((3, chunks)), dma((3, chunks)),
            dma((chunks,)), dma((chunks,)), dma((21,)), dma((21,)), dma((4,)), dma((2, 2)),
        ],
        compiler_params=pltpu.CompilerParams(
            collective_id=0, has_side_effects=True, vmem_limit_bytes=63 * 1024 * 1024
        ),
    )(pair_density.reshape(width, waves), coulomb)


def solution(mesh):
    in_specs = (P("ka", None, "ga"), P("ga"))
    out_specs = P(("ka", "ga"), None)
    body = functools.partial(shards, mesh.shape["ka"])
    return jax.shard_map(body, mesh=mesh, in_specs=in_specs, out_specs=out_specs, check_vma=False)
```
